32 devices in a mesh: ctx: 8 (over z, x), head: 4 (over y, core).
Axes of the slice: x: 2, y: 2, z: 4, core: 2. Of those that a mesh axis runs over, the one named last changes fastest.
Arguments:
- hidden: bfloat16 [256, 8192], P(None, 'ctx')
- norm_gain: float32 [8192], replicated, may hold values from 0.1 to 1.9
- w_query: bfloat16 [8192, 8192], P('ctx', 'head'), may hold values from -0.0625 to 0.0625
- manifest_keys: bfloat16 [8, 4096, 128], P(None, 'ctx')
- manifest_values: bfloat16 [8, 4096, 128], P(None, 'ctx'), may hold values from -6 to 6
- w_output: bfloat16 [8192, 8192], P('head', 'ctx'), may hold values from -0.0625 to 0.0625
- valid_len: int32 [256], replicated, may hold values from 1 to 4096, as said below
- home_block: int32 [256], replicated, may hold values from 0 to 7, as said below
Outputs:
- projected: float32 [256, 8192], P('head', 'ctx')
The draws below stay inside these ranges and needn't reach their ends.
Inputs may be any that keep to these rules, and one draw needn't show every extreme that they name: `valid_len`: every draw has a row that reads the whole manifest and a row with length 1. `home_block`: every draw assigns some row to the first block and some row to the last.
All inputs are finite; a program needn't handle non-finite values.
Results may differ from the reference program's by a relative error of at most 0.005.
The reference program's roundings to bfloat16 on the way count: a program that leaves them out, or rounds other values in their place, can miss the bound.
Values may be sent and summed in bfloat16 or wider, within the bound.
A program may use at most 128 MiB of HBM per device.

```python
import math
import jax
import jax.numpy as jnp
from jax import lax

D = 8192
H = 64
KVH = 8
HD = 128
L_DEV = 512
ROWS = 256
CTXLEN = 4096
NBLK = 8
GROUP = 8


def draw_hidden(key, part):
    key_base, key_rows, key_cols = jax.random.split(key, 3)
    base = jax.random.normal(key_base, (ROWS, D), jnp.float32)
    row_scale = jnp.exp(jax.random.uniform(key_rows, (ROWS, 1), jnp.float32, 0.0, math.log(10.0)))
    ramp = jnp.exp(math.log(3.0) * jnp.arange(D, dtype=jnp.float32) / D)
    col_scale = jnp.exp(jax.random.uniform(key_cols, (1, D), jnp.float32, 0.0, math.log(5.0))) * ramp[None, :]
    return (base * row_scale * col_scale).astype(jnp.bfloat16)


def draw_manifest_keys(key, part):
    key_base = jax.random.fold_in(key, 0)
    result = jax.random.normal(key_base, (KVH, CTXLEN, HD), jnp.float32) * 3.0
    return result.astype(jnp.bfloat16)


def draw_valid_len(key, part):
    key_len, key_pick = jax.random.split(key, 2)
    lengths = jax.random.randint(key_len, (ROWS,), 1, CTXLEN + 1)
    picked = jax.random.randint(key_pick, (), 0, ROWS)
    lengths = lengths.at[picked].set(CTXLEN)
    lengths = lengths.at[(picked + 1) % ROWS].set(1)
    return lengths.astype(jnp.int32)


def draw_home_block(key, part):
    key_block, key_pick = jax.random.split(key, 2)
    blocks = jax.random.randint(key_block, (ROWS,), 0, NBLK)
    picked = jax.random.randint(key_pick, (), 0, ROWS)
    blocks = blocks.at[picked].set(0)
    blocks = blocks.at[(picked + 1) % ROWS].set(NBLK - 1)
    return blocks.astype(jnp.int32)


def levels(rng, extent, cuts, low, largest):
    def one(position, blocks):
        draws = jax.random.uniform(jax.random.fold_in(jax.random.fold_in(rng, 6), position), (blocks,), jnp.float32, low / len(cuts), largest / len(cuts))
        return jnp.repeat(jnp.exp(draws), extent[position] // blocks).reshape((-1,) + (1,) * (len(extent) - position - 1))

    factor_of = one(*cuts[0])
    for cut in cuts[1:]:
        factor_of = factor_of * one(*cut)
    return factor_of


def gaussian(stream_key, shape, deviation, limit, shards=(), kind=jnp.bfloat16):
    values = deviation * jax.random.normal(stream_key, shape, jnp.float32)
    if shards:
        values = values * levels(stream_key, shape, shards, -0.22, 0.18)
    return jnp.clip(values, -limit, limit).astype(kind)


def setup_inputs(seed: int = 0) -> dict:
    key_of = jax.random.split(jax.random.key(seed), 9)
    return {
        "hidden": draw_hidden(jax.random.fold_in(key_of[8], 71), 0),
        "norm_gain": jnp.clip(1.0 + 0.18 * jax.random.normal(key_of[1], (D,), jnp.float32), 0.1, 1.9),
        "w_query": gaussian(key_of[2], (D, H * HD), D ** -0.5, 0.0625, ((0, 8), (1, 4))),
        "manifest_keys": draw_manifest_keys(jax.random.fold_in(key_of[8], 71), 0),
        "manifest_values": gaussian(key_of[4], (KVH, CTXLEN, HD), 1.0, 6.0, ((1, 8),)),
        "w_output": gaussian(key_of[5], (H * HD, D), (H * HD) ** -0.5, 0.0625, ((0, 4), (1, 8))),
        "valid_len": draw_valid_len(jax.random.fold_in(key_of[8], 71), 0),
        "home_block": draw_home_block(jax.random.fold_in(key_of[8], 71), 0),
    }


def reference(hidden, norm_gain, w_query, manifest_keys, manifest_values, w_output, valid_len, home_block):
    widened = hidden.astype(jnp.float32)
    inv_rms = lax.rsqrt(lax.optimization_barrier(jnp.mean(widened * widened, axis=1, keepdims=True)) + 1e-05)
    normed = (widened * inv_rms * norm_gain[None, :]).astype(jnp.bfloat16)
    query = jnp.dot(normed, w_query, preferred_element_type=jnp.float32).astype(jnp.bfloat16)
    places = jnp.arange(CTXLEN, dtype=jnp.int32)
    usable = (places[None, :] < valid_len[:, None]) | ((places // L_DEV)[None, :] == home_block[:, None])
    by_head = query.reshape(ROWS, H, HD).transpose(1, 0, 2)

    def one_head(head_index):
        q_head = lax.dynamic_index_in_dim(by_head, head_index, 0, keepdims=False)
        kv_index = (head_index // GROUP).astype(jnp.int32)
        key_head = lax.dynamic_index_in_dim(manifest_keys, kv_index, 0, keepdims=False)
        value_head = lax.dynamic_index_in_dim(manifest_values, kv_index, 0, keepdims=False)
        scores = jnp.dot(q_head, key_head.T, preferred_element_type=jnp.float32) * (1.0 / math.sqrt(HD))
        scores = jnp.where(usable, scores, -1e+30)
        row_max = lax.optimization_barrier(jnp.max(scores, axis=1, keepdims=True))
        expo_vals = jnp.where(usable, jnp.exp(scores - row_max), 0.0)
        row_sum = lax.optimization_barrier(jnp.sum(expo_vals, axis=1, keepdims=True))
        weighted = jnp.dot(expo_vals.astype(jnp.bfloat16), value_head, preferred_element_type=jnp.float32)
        return (weighted / row_sum).astype(jnp.bfloat16)
    attn = lax.map(one_head, jnp.arange(H, dtype=jnp.int32))
    attn = attn.transpose(1, 0, 2).reshape(ROWS, H * HD)
    return jnp.dot(attn, w_output, preferred_element_type=jnp.float32)
```

```python
import math

import jax
import jax.numpy as jnp
from jax import lax
from jax.experimental import pallas as pl
from jax.experimental.pallas import tpu as pltpu
from jax.sharding import PartitionSpec as P

H = 64
KVH = 8
HD = 128

Z = 4
X = 2
PARTS = 2
NSEM = 128

MESH = pl.DeviceIdType.MESH
f32, bf16, i16, i32 = jnp.float32, jnp.bfloat16, jnp.int16, jnp.int32


def fused_kernel(
    hidden_hbm, gain_hbm, wq_hbm, k_hbm, v_hbm, wo_hbm, lens_hbm, home_hbm, out,
    hid, gain, wq, wo, lens, home, kv, vt, nrm, sq,
    xs, xss, xr, xrs, own, zls, zlss, zlr, zlrs, locs, locr, fin, fins, finr, finrs, mine,
    qb, sc, os_, st, oqs, oss, oqr, osr, az, ag, acc, cr, ys, yr,
    local_sem, send_sem, recv_sem,
):
    c = lax.axis_index("ctx")
    h = lax.axis_index("head")
    z, x = lax.div(c, X), lax.rem(c, X)
    y, b = lax.div(h, 2), lax.rem(h, 2)
    zb, zh = lax.rem(z, 2), lax.div(z, 2)
    nz = lax.axis_size("ctx")
    rows, feat = hid.shape
    rp = rows // PARTS
    span = kv.shape[2]
    chunk = wq.shape[1] // nz
    scale = 1.0 / math.sqrt(HD)
    is_o = b == zb
    is_f = b != zb
    pending = []
    sems = {"send": 0, "recv": 0}
    names = {}

    def at(zz, xx):
        return zz * X + xx

    def recv_index(name, count=1):
        if name not in names:
            names[name] = sems["recv"]
            sems["recv"] += count
        return names[name]

    def run(cond, fn):
        if cond is None:
            fn()
        else:
            pl.when(cond)(fn)

    def send(src, dst, where, recv, cond=None):
        i = sems["send"]
        sems["send"] += 1
        copy = pltpu.make_async_remote_copy(
            src_ref=src, dst_ref=dst, send_sem=send_sem.at[i], recv_sem=recv_sem.at[recv],
            device_id=where, device_id_type=MESH,
        )
        run(cond, copy.start)
        pending.append((cond, copy))

    def wait(dst, recv, cond=None):
        copy = pltpu.make_async_remote_copy(
            src_ref=dst, dst_ref=dst, send_sem=send_sem.at[0], recv_sem=recv_sem.at[recv],
            device_id={"ctx": at(z, 1 - x)}, device_id_type=MESH,
        )
        run(cond, copy.wait_recv)

    beside = {"ctx": at(z, 1 - x)}
    twin = {"head": y * 2 + 1 - b}
    over = {"head": (1 - y) * 2 + b}

    def key_head(zz):
        return 4 * y + 2 * lax.rem(zz, 2) + lax.div(zz, 2)

    z_near = z + 1 - 2 * zb
    z_far = 3 - z
    z_two = lax.rem(z + 2, Z)

    def on_core(zz, core):
        return {"ctx": at(zz, x), "head": y * 2 + core}

    loads = [
        pltpu.make_async_copy(hidden_hbm, hid, local_sem.at[0]),
        pltpu.make_async_copy(gain_hbm.at[:, pl.ds(pl.multiple_of(c * feat, feat), feat)], gain, local_sem.at[1]),
        pltpu.make_async_copy(wq_hbm, wq, local_sem.at[2]),
        pltpu.make_async_copy(k_hbm.at[key_head(z)], kv.at[0, z], local_sem.at[3]),
        pltpu.make_async_copy(v_hbm.at[key_head(z)], kv.at[1, z], local_sem.at[4]),
        pltpu.make_async_copy(lens_hbm, lens, local_sem.at[5]),
        pltpu.make_async_copy(home_hbm, home, local_sem.at[6]),
        pltpu.make_async_copy(wo_hbm, wo, local_sem.at[7]),
    ]
    for cp in loads:
        cp.start()

    barrier = pltpu.get_barrier_semaphore()
    peers = [{"ctx": lax.rem(c + k, nz)} for k in range(1, nz)]
    peers += [on_core(zz, 1 - b) for zz in (z_near, z_far, z_two)]
    peers += [twin, over]
    for peer in peers:
        pl.semaphore_signal(barrier, inc=1, device_id=peer, device_id_type=MESH)

    loads[0].wait()
    eye = lax.broadcasted_iota(i32, (128, 128), 0) == lax.broadcasted_iota(i32, (128, 128), 1)
    wide = hid[...].astype(f32)
    col = jnp.sum(wide * wide, axis=1, keepdims=True)
    pieces = [
        jnp.sum(jnp.where(eye, col[i * 128 : (i + 1) * 128], 0.0), axis=0, keepdims=True)
        for i in range(rows // 128)
    ]
    pieces.append(jnp.zeros((8 - rows // 128, 128), f32))
    sq[0] = jnp.concatenate(pieces, axis=0)
    pl.semaphore_wait(barrier, len(peers))
    sq_sem = recv_index("sq", nz)
    for k in range(1, nz):
        send(sq.at[0], sq.at[k], {"ctx": lax.rem(c + k, nz)}, sq_sem + k)

    kv_sem = recv_index("kv", Z)
    kvf_sem = recv_index("kvf", Z)
    for zz in (z_far, z_two, z_near):
        for core, hbm in ((0, k_hbm), (1, v_hbm)):
            send(hbm.at[key_head(zz)], kv.at[core, z], {"ctx": at(zz, x)}, kv_sem + z, b == core)

    def share(zz):
        wait(kv.at[b, zz], kv_sem + zz)
        send(kv.at[b, zz], kv.at[b, zz], twin, kvf_sem + zz)

    loads[1].wait()
    for k in range(1, nz):
        wait(sq.at[k], sq_sem + k)
    total = sq[0]
    for k in range(1, nz):
        total = total + sq[k]
    inv = lax.rsqrt(total / (feat * nz) + 1e-05)

    def normalise(i):
        part = slice(i * 128, (i + 1) * 128)
        inv_col = jnp.sum(jnp.where(eye, inv[i : i + 1, :], 0.0), axis=1, keepdims=True)
        nrm[part, :] = (hid[part, :].astype(f32) * inv_col * gain[...]).astype(bf16)

    def pack(value):
        top = jnp.maximum(jnp.max(jnp.abs(value), axis=0, keepdims=True), 1e-30)
        code = jnp.round(value * (32766.0 / top)).astype(i32).astype(i16)
        return code, top * (1.0 / 32766.0)

    def unpack(code, factor):
        return code.astype(i32).astype(f32) * factor

    cross, near = 1 - zh, zh
    targets = (cross, near)

    def partial(r, zz, xx):
        first = pl.multiple_of(zz * 4 * chunk + xx * 2 * chunk, 2 * chunk)
        return jnp.dot(nrm[r * rp : (r + 1) * rp, :], wq[:, pl.ds(first, 2 * chunk)], preferred_element_type=f32)

    def project_out(r):
        for i, zz in enumerate(targets):
            xs[r, i], xss[r, i] = pack(partial(r, zz, 1 - x))
            send(xss.at[r, i], xrs.at[r, i], beside, recv_index(("xs", r, i)))
            send(xs.at[r, i], xr.at[r, i], beside, recv_index(("x", r, i)))

    def project_own(r):
        for i, zz in enumerate(targets):
            own[r, i] = partial(r, zz, x)

    def x_sum(r, i):
        wait(xrs.at[r, i], recv_index(("xs", r, i)))
        wait(xr.at[r, i], recv_index(("x", r, i)))
        own[r, i] = own[r, i] + unpack(xr[r, i], xrs[r, i])

    def send_final(r, i, value, zz, kind):
        code, factor = pack(value)
        for core in range(2):
            fin[r, i, core] = code[:, core * chunk : (core + 1) * chunk]
            fins[r, i, core] = factor[:, core * chunk : (core + 1) * chunk]

    def start_final(r, i, zz, kind):
        for core in range(2):
            where = on_core(zz, core)
            send(fins.at[r, i, core], finrs.at[r, i], where, recv_index(("fs", r, i)), is_f)
            send(fin.at[r, i, core], finr.at[r, i], where, recv_index(("f", r, i)), is_f)

    def cross_first(r):
        x_sum(r, 0)

        def go():
            zls[r], zlss[r] = pack(own[r, 0])

        pl.when(is_o)(go)
        where = {"ctx": at(z_near, x)}
        send(zlss.at[r], zlrs.at[r], where, recv_index(("zls", r)), is_o)
        send(zls.at[r], zlr.at[r], where, recv_index(("zl", r)), is_o)

    def cross_second(r):
        wait(zlrs.at[r], recv_index(("zls", r)), is_f)
        wait(zlr.at[r], recv_index(("zl", r)), is_f)

        def go():
            send_final(r, 0, own[r, 0] + unpack(zlr[r], zlrs[r]), z_far, "cross")

        pl.when(is_f)(go)
        start_final(r, 0, z_far, "cross")

    def near_step(r):
        x_sum(r, 1)

        def keep():
            for core in range(2):

                def half():
                    mine[r] = own[r, 1, :, core * chunk : (core + 1) * chunk]
                    locs[r] = own[r, 1, :, (1 - core) * chunk : (2 - core) * chunk]

                pl.when(b == core)(half)

        pl.when(is_o)(keep)
        send(locs.at[r], locr.at[r], twin, recv_index(("loc", r)), is_o)
        pl.when(is_f)(lambda: send_final(r, 1, own[r, 1], z_near, "near"))
        start_final(r, 1, z_near, "near")

    def query(r):
        wait(locr.at[r], recv_index(("loc", r)), is_f)

        def take():
            mine[r] = locr[r]

        pl.when(is_f)(take)
        total = mine[r]
        for i in (1, 0):
            wait(finrs.at[r, i], recv_index(("fs", r, i)))
            wait(finr.at[r, i], recv_index(("f", r, i)))
            total = total + unpack(finr[r, i], finrs[r, i])
        q = total.astype(bf16)
        for j in range(2):
            qb[0, r, j * rp : (j + 1) * rp, :] = q[:, j * HD : (j + 1) * HD]
        send(qb.at[0, r], qb.at[1, r], beside, recv_index(("q", r)))

    place = lax.broadcasted_iota(i32, (span, 2 * rp), 0)

    def attend(i, r):
        part = slice(r * rp, (r + 1) * rp)
        if i == 1:
            wait(qb.at[1, r], recv_index(("q", r)))
        home_r = jnp.concatenate([home[:, part]] * 2, axis=1)
        lens_r = jnp.concatenate([lens[:, part]] * 2, axis=1)
        top = jnp.full((1, 2 * rp), -1e30, f32)
        for s in range(Z):
            block = at(s, x)
            limit = jnp.where(home_r == block, span, lens_r - block * span)
            raw = lax.dot_general(kv[0, s], qb[i, r], (((1,), (1,)), ((), ())), preferred_element_type=f32)
            raw = jnp.where(place < limit, raw, -1e30)
            sc[s] = raw
            top = jnp.maximum(top, jnp.max(raw, axis=0, keepdims=True))
        tot = jnp.zeros((1, 2 * rp), f32)
        acc_o = jnp.zeros((HD, 2 * rp), f32)
        for s in range(Z):
            e = jnp.exp((sc[s] - top) * scale)
            tot = tot + jnp.sum(e, axis=0, keepdims=True)
            acc_o = acc_o + jnp.dot(vt[s], e.astype(bf16), preferred_element_type=f32)
        if i == 0:
            os_[r] = acc_o
            st[r, 0:1, :] = top
            st[r, 1:2, :] = tot
        else:
            code, factor = pack(acc_o)
            oqs[r] = code
            oss[r, 0:1, :] = top
            oss[r, 1:2, :] = tot
            oss[r, 2:3, :] = factor
            oss[r, 3:4, :] = factor
            send(oss.at[r], osr.at[r], beside, recv_index(("os", r)))
            send(oqs.at[r], oqr.at[r], beside, recv_index(("o", r)))

    ag_sem = [recv_index(("ag", r), 8) for r in range(PARTS)]

    def slot(zz, xx, core):
        return zz * 4 + xx * 2 + core

    def merge(r):
        wait(osr.at[r], recv_index(("os", r)))
        wait(oqr.at[r], recv_index(("o", r)))
        m0, m1 = st[r, 0:1, :], osr[r, 0:1, :]
        l0, l1 = st[r, 1:2, :], osr[r, 1:2, :]
        m = jnp.maximum(m0, m1)
        a0, a1 = jnp.exp((m0 - m) * scale), jnp.exp((m1 - m) * scale)
        res = (a0 * os_[r] + unpack(oqr[r], a1 * osr[r, 2:3, :])) / (a0 * l0 + a1 * l1)
        turned = res.T.astype(bf16)
        for j in range(2):
            az[r, :, j * HD : (j + 1) * HD] = turned[j * rp : (j + 1) * rp, :]
        mine_slot = slot(zh, x, b)

        def keep():
            ag[r, mine_slot] = az[r]

        pl.when(is_o)(keep)
        send(az.at[r], ag.at[r, mine_slot], twin, ag_sem[r] + mine_slot, is_f)
        for zz in (z_far, z_two, z_near):
            send(az.at[r], ag.at[r, mine_slot], on_core(zz, zb), ag_sem[r] + mine_slot)

    def product(r, s):
        first = pl.multiple_of(s * chunk, chunk)
        return jnp.dot(ag[r, s], wo[pl.ds(first, chunk), :], preferred_element_type=f32)

    def relay(r, zz, first=False):
        part = slice(r * rp, (r + 1) * rp)
        for core in range(2):
            s = slot(zz, x, core)
            if zz is near:
                wait(ag.at[r, s], ag_sem[r] + s, jnp.logical_not(jnp.logical_and(is_o, b == core)))
            else:
                wait(ag.at[r, s], ag_sem[r] + s)
            send(ag.at[r, s], ag.at[r, s], beside, ag_sem[r] + s)
        value = product(r, slot(zz, x, 0)) + product(r, slot(zz, x, 1))
        if first:
            acc[part, :] = value
        else:
            acc[part, :] += value

    def collect(r, zz):
        part = slice(r * rp, (r + 1) * rp)
        for core in range(2):
            s = slot(zz, 1 - x, core)
            wait(ag.at[r, s], ag_sem[r] + s)
        acc[part, :] += product(r, slot(zz, 1 - x, 0)) + product(r, slot(zz, 1 - x, 1))

    quarter = out.shape[0]

    def rows_of(t, core):
        return pl.ds(pl.multiple_of(t * 2 * quarter + core * quarter, quarter), quarter)

    def reduce_cores(t):
        send(acc.at[rows_of(t, 1 - b), :], cr.at[t], twin, recv_index(("c", t)))

    def reduce_chips(t):
        wait(cr.at[t], recv_index(("c", t)))

        def away():
            ys[...] = (acc[rows_of(t, b), :] + cr[t]).astype(bf16)

        pl.when(y != t)(away)
        send(ys, yr, over, recv_index("y"), y != t)

    def finish(t):
        def here():
            out[...] = acc[rows_of(t, b), :] + cr[t] + yr[...].astype(f32)

        wait(yr, recv_index("y"), y == t)
        pl.when(y == t)(here)

    normalise(0)
    loads[2].wait()
    project_out(0)
    normalise(1)
    project_out(1)
    project_own(0)
    project_own(1)
    share(z_near)
    cross_first(0)
    cross_second(0)
    near_step(0)
    share(z_two)
    share(z_far)
    cross_first(1)
    query(0)
    for cp in loads[3:]:
        cp.wait()
    for zz in (z_near, z_two, z_far):
        wait(kv.at[1 - b, zz], kvf_sem + zz)
    for s in range(Z):
        vt[s] = kv[1, s].astype(f32).T.astype(bf16)
    attend(0, 0)
    cross_second(1)
    near_step(1)
    attend(1, 0)
    query(1)
    attend(0, 1)
    merge(0)
    attend(1, 1)
    relay(0, near, True)
    relay(0, cross)
    merge(1)
    relay(1, near, True)
    collect(0, near)
    collect(0, cross)
    reduce_cores(0)
    relay(1, cross)
    reduce_chips(0)
    collect(1, near)
    collect(1, cross)
    reduce_cores(1)
    finish(0)
    reduce_chips(1)
    finish(1)
    for cond, cp in pending:
        run(cond, cp.wait_send)


def fused(hidden, norm_gain, w_query, keys, values, w_output, valid_len, home_block):
    rows, feat = hidden.shape
    cols = w_output.shape[1]
    nz, nh = lax.axis_size("ctx"), lax.axis_size("head")
    span = keys.shape[1]
    chunk = w_query.shape[1] // nz
    rp = rows // PARTS
    quarter = rows // nh
    hbm = pl.BlockSpec(memory_space=pltpu.HBM)
    return pl.pallas_call(
        fused_kernel,
        out_shape=jax.ShapeDtypeStruct((quarter, cols), f32),
        in_specs=[hbm] * 8,
        out_specs=pl.BlockSpec(memory_space=pltpu.VMEM),
        scratch_shapes=[
            pltpu.VMEM((rows, feat), bf16),
            pltpu.VMEM((1, feat), f32),
            pltpu.VMEM(w_query.shape, bf16),
            pltpu.VMEM(w_output.shape, bf16),
            pltpu.VMEM((1, rows), i32),
            pltpu.VMEM((1, rows), i32),
            pltpu.VMEM((2, Z, span, HD), bf16),
            pltpu.VMEM((Z, HD, span), bf16),
            pltpu.VMEM((rows, feat), bf16),
            pltpu.VMEM((nz, 8, 128), f32),
            pltpu.VMEM((PARTS, 2, rp, 2 * chunk), i16),
            pltpu.VMEM((PARTS, 2, 1, 2 * chunk), f32),
            pltpu.VMEM((PARTS, 2, rp, 2 * chunk), i16),
            pltpu.VMEM((PARTS, 2, 1, 2 * chunk), f32),
            pltpu.VMEM((PARTS, 2, rp, 2 * chunk), f32),
            pltpu.VMEM((PARTS, rp, 2 * chunk), i16),
            pltpu.VMEM((PARTS, 1, 2 * chunk), f32),
            pltpu.VMEM((PARTS, rp, 2 * chunk), i16),
            pltpu.VMEM((PARTS, 1, 2 * chunk), f32),
            pltpu.VMEM((PARTS, rp, chunk), f32),
            pltpu.VMEM((PARTS, rp, chunk), f32),
            pltpu.VMEM((PARTS, 2, 2, rp, chunk), i16),
            pltpu.VMEM((PARTS, 2, 2, 1, chunk), f32),
            pltpu.VMEM((PARTS, 2, rp, chunk), i16),
            pltpu.VMEM((PARTS, 2, 1, chunk), f32),
            pltpu.VMEM((PARTS, rp, chunk), f32),
            pltpu.VMEM((2, PARTS, 2 * rp, HD), bf16),
            pltpu.VMEM((Z, span, 2 * rp), f32),
            pltpu.VMEM((PARTS, HD, 2 * rp), f32),
            pltpu.VMEM((PARTS, 8, 2 * rp), f32),
            pltpu.VMEM((PARTS, HD, 2 * rp), i16),
            pltpu.VMEM((PARTS, 4, 2 * rp), f32),
            pltpu.VMEM((PARTS, HD, 2 * rp), i16),
            pltpu.VMEM((PARTS, 4, 2 * rp), f32),
            pltpu.VMEM((PARTS, rp, chunk), bf16),
            pltpu.VMEM((PARTS, nz, rp, chunk), bf16),
            pltpu.VMEM((rows, cols), f32),
            pltpu.VMEM((2, quarter, cols), f32),
            pltpu.VMEM((quarter, cols), bf16),
            pltpu.VMEM((quarter, cols), bf16),
            pltpu.SemaphoreType.DMA((8,)),
            pltpu.SemaphoreType.DMA((NSEM,)),
            pltpu.SemaphoreType.DMA((NSEM,)),
        ],
        compiler_params=pltpu.CompilerParams(
            collective_id=0, has_side_effects=True, vmem_limit_bytes=60 * 1024 * 1024
        ),
    )(
        hidden, norm_gain.reshape(1, -1), w_query, keys, values, w_output,
        valid_len.reshape(1, -1), home_block.reshape(1, -1),
    )


def shards(
    hidden, norm_gain, w_query, manifest_keys, manifest_values, w_output, valid_len, home_block
):
    ctx_count = lax.axis_size("ctx")
    ctx_index = lax.axis_index("ctx")
    head_index = lax.axis_index("head")
    rows, feat = hidden.shape
    d_model = feat * ctx_count
    width = w_query.shape[1]
    heads_here = width // HD
    group = H // KVH
    span = manifest_keys.shape[1]
    hsplit = min(ctx_count, heads_here)
    rsplit = ctx_count // hsplit
    rows_dev = rows // rsplit
    heads_dev = heads_here // hsplit

    widened = hidden.astype(jnp.float32)
    total_sq = lax.psum(jnp.sum(widened * widened, axis=1, keepdims=True), "ctx")
    inv_rms = lax.rsqrt(total_sq / d_model + 1e-05)
    gain = lax.dynamic_slice_in_dim(norm_gain, ctx_index * feat, feat, 0)
    normed = (widened * inv_rms * gain[None, :]).astype(jnp.bfloat16)
    partial = jnp.dot(normed, w_query, preferred_element_type=jnp.float32)
    partial = partial.reshape(rsplit, rows_dev, hsplit, heads_dev * HD).transpose(2, 0, 1, 3)
    partial = partial.reshape(ctx_count, rows_dev, heads_dev * HD)
    query = lax.psum_scatter(partial, "ctx", scatter_dimension=0, tiled=False).astype(jnp.bfloat16)

    dest_heads = head_index * heads_here + (jnp.arange(ctx_count) // rsplit) * heads_dev
    dest_kv = dest_heads // group
    kv = jnp.stack(
        [
            jnp.stack([lax.dynamic_index_in_dim(a, dest_kv[i], 0, keepdims=False) for a in (manifest_keys, manifest_values)])
            for i in range(ctx_count)
        ]
    )
    kv = lax.all_to_all(kv, "ctx", split_axis=0, concat_axis=0, tiled=True)
    kv = kv.transpose(1, 0, 2, 3).reshape(2, ctx_count * span, HD)
    keys, values = kv[0], kv[1]

    first_row = (ctx_index % rsplit) * rows_dev
    lens = lax.dynamic_slice_in_dim(valid_len, first_row, rows_dev, 0)
    blocks = lax.dynamic_slice_in_dim(home_block, first_row, rows_dev, 0)
    places = jnp.arange(ctx_count * span, dtype=jnp.int32)
    usable = (places[None, :] < lens[:, None]) | ((places // span)[None, :] == blocks[:, None])
    usable = usable[:, None, :]
    q3 = query.reshape(rows_dev, heads_dev, HD)
    scores = jnp.einsum("nhd,jd->nhj", q3, keys, preferred_element_type=jnp.float32) * (
        1.0 / math.sqrt(HD)
    )
    scores = jnp.where(usable, scores, -1e30)
    row_max = jnp.max(scores, axis=2, keepdims=True)
    expo = jnp.where(usable, jnp.exp(scores - row_max), 0.0)
    row_sum = jnp.sum(expo, axis=2, keepdims=True)
    weighted = jnp.einsum(
        "nhj,jd->nhd", expo.astype(jnp.bfloat16), values, preferred_element_type=jnp.float32
    )
    attn = (weighted / row_sum).astype(jnp.bfloat16).reshape(rows_dev, heads_dev * HD)
    attn = lax.all_gather(attn, "ctx", axis=0, tiled=False)
    attn = attn.reshape(hsplit, rsplit, rows_dev, heads_dev * HD).transpose(1, 2, 0, 3)
    attn = attn.reshape(rows, width)
    return lax.psum_scatter(
        jnp.dot(attn, w_output, preferred_element_type=jnp.float32),
        "head",
        scatter_dimension=0,
        tiled=True,
    )


def solution(mesh):
    in_specs = (
        P(None, "ctx"),
        P(),
        P("ctx", "head"),
        P(None, "ctx", None),
        P(None, "ctx", None),
        P("head", "ctx"),
        P(),
        P(),
    )
    out_specs = P("head", "ctx")
    small = mesh.shape["ctx"] == Z * X and mesh.shape["head"] * X == KVH
    return jax.shard_map(fused if small else shards, mesh=mesh, in_specs=in_specs, out_specs=out_specs, check_vma=False)
```

```python
import math

import jax
import jax.numpy as jnp
from jax import lax
from jax.experimental import pallas as pl
from jax.experimental.pallas import tpu as pltpu
from jax.sharding import PartitionSpec as P

H = 64
KVH = 8
HD = 128

Z = 4
X = 2
PARTS = 2
NSEM = 128

MESH = pl.DeviceIdType.MESH
f32, bf16, i16, i32 = jnp.float32, jnp.bfloat16, jnp.int16, jnp.int32


def fused_kernel(
    hidden_hbm, gain_hbm, wq_hbm, k_hbm, v_hbm, wo_hbm, lens_hbm, home_hbm, out,
    hid, gain, wq, wo, lens, home, kv, vt, nrm, sq,
    xs, xss, xr, xrs, own, zls, zlss, zlr, zlrs, locs, locr, fin, fins, finr, finrs, mine,
    qb, sc, os_, st, oqs, oss, oqr, osr, az, ag, acc, cr, ys, yr,
    local_sem, send_sem, recv_sem,
):
    c = lax.axis_index("ctx")
    h = lax.axis_index("head")
    z, x = lax.div(c, X), lax.rem(c, X)
    y, b = lax.div(h, 2), lax.rem(h, 2)
    zb, zh = lax.rem(z, 2), lax.div(z, 2)
    nz = lax.axis_size("ctx")
    rows, feat = hid.shape
    rp = rows // PARTS
    span = kv.shape[2]
    chunk = wq.shape[1] // nz
    scale = 1.0 / math.sqrt(HD)
    is_o = b == zb
    is_f = b != zb
    pending = []
    sems = {"send": 0, "recv": 0}
    names = {}

    def at(zz, xx):
        return zz * X + xx

    def recv_index(name, count=1):
        if name not in names:
            names[name] = sems["recv"]
            sems["recv"] += count
        return names[name]

    def run(cond, fn):
        if cond is None:
            fn()
        else:
            pl.when(cond)(fn)

    def send(src, dst, where, recv, cond=None):
        i = sems["send"]
        sems["send"] += 1
        copy = pltpu.make_async_remote_copy(
            src_ref=src, dst_ref=dst, send_sem=send_sem.at[i], recv_sem=recv_sem.at[recv],
            device_id=where, device_id_type=MESH,
        )
        run(cond, copy.start)
        pending.append((cond, copy))

    def wait(dst, recv, cond=None):
        copy = pltpu.make_async_remote_copy(
            src_ref=dst, dst_ref=dst, send_sem=send_sem.at[0], recv_sem=recv_sem.at[recv],
            device_id={"ctx": at(z, 1 - x)}, device_id_type=MESH,
        )
        run(cond, copy.wait_recv)

    beside = {"ctx": at(z, 1 - x)}
    twin = {"head": y * 2 + 1 - b}
    over = {"head": (1 - y) * 2 + b}

    def key_head(zz):
        return 4 * y + 2 * lax.rem(zz, 2) + lax.div(zz, 2)

    z_near = z + 1 - 2 * zb
    z_far = 3 - z
    z_two = lax.rem(z + 2, Z)

    def on_core(zz, core):
        return {"ctx": at(zz, x), "head": y * 2 + core}

    loads = [
        pltpu.make_async_copy(hidden_hbm, hid, local_sem.at[0]),
        pltpu.make_async_copy(gain_hbm.at[:, pl.ds(pl.multiple_of(c * feat, feat), feat)], gain, local_sem.at[1]),
        pltpu.make_async_copy(wq_hbm, wq, local_sem.at[2]),
        pltpu.make_async_copy(k_hbm.at[key_head(z)], kv.at[0, z], local_sem.at[3]),
        pltpu.make_async_copy(v_hbm.at[key_head(z)], kv.at[1, z], local_sem.at[4]),
        pltpu.make_async_copy(lens_hbm, lens, local_sem.at[5]),
        pltpu.make_async_copy(home_hbm, home, local_sem.at[6]),
        pltpu.make_async_copy(wo_hbm, wo, local_sem.at[7]),
    ]
    for cp in loads:
        cp.start()

    barrier = pltpu.get_barrier_semaphore()
    peers = [{"ctx": lax.rem(c + k, nz)} for k in range(1, nz)]
    peers += [on_core(zz, 1 - b) for zz in (z_near, z_far, z_two)]
    peers += [twin, over]
    for peer in peers:
        pl.semaphore_signal(barrier, inc=1, device_id=peer, device_id_type=MESH)

    loads[0].wait()
    eye = lax.broadcasted_iota(i32, (128, 128), 0) == lax.broadcasted_iota(i32, (128, 128), 1)
    wide = hid[...].astype(f32)
    col = jnp.sum(wide * wide, axis=1, keepdims=True)
    pieces = [
        jnp.sum(jnp.where(eye, col[i * 128 : (i + 1) * 128], 0.0), axis=0, keepdims=True)
        for i in range(rows // 128)
    ]
    pieces.append(jnp.zeros((8 - rows // 128, 128), f32))
    sq[0] = jnp.concatenate(pieces, axis=0)
    pl.semaphore_wait(barrier, len(peers))
    sq_sem = recv_index("sq", nz)
    for k in range(1, nz):
        send(sq.at[0], sq.at[k], {"ctx": lax.rem(c + k, nz)}, sq_sem + k)

    kv_sem = recv_index("kv", Z)
    kvf_sem = recv_index("kvf", Z)
    def give(zz):
        for core, hbm in ((0, k_hbm), (1, v_hbm)):
            send(hbm.at[key_head(zz)], kv.at[core, z], {"ctx": at(zz, x)}, kv_sem + z, b == core)

    def share(zz):
        wait(kv.at[b, zz], kv_sem + zz)
        send(kv.at[b, zz], kv.at[b, zz], twin, kvf_sem + zz)

    loads[1].wait()
    for k in range(1, nz):
        wait(sq.at[k], sq_sem + k)
    total = sq[0]
    for k in range(1, nz):
        total = total + sq[k]
    inv = lax.rsqrt(total / (feat * nz) + 1e-05)

    def normalise(i):
        part = slice(i * 128, (i + 1) * 128)
        inv_col = jnp.sum(jnp.where(eye, inv[i : i + 1, :], 0.0), axis=1, keepdims=True)
        nrm[part, :] = (hid[part, :].astype(f32) * inv_col * gain[...]).astype(bf16)

    def pack(value):
        top = jnp.maximum(jnp.max(jnp.abs(value), axis=0, keepdims=True), 1e-30)
        code = jnp.round(value * (32766.0 / top)).astype(i32).astype(i16)
        return code, top * (1.0 / 32766.0)

    def unpack(code, factor):
        return code.astype(i32).astype(f32) * factor

    cross, near = 1 - zh, zh
    targets = (cross, near)

    def partial(r, zz, xx):
        first = pl.multiple_of(zz * 4 * chunk + xx * 2 * chunk, 2 * chunk)
        return jnp.dot(nrm[r * rp : (r + 1) * rp, :], wq[:, pl.ds(first, 2 * chunk)], preferred_element_type=f32)

    def project_out(r):
        for i, zz in enumerate(targets):
            xs[r, i], xss[r, i] = pack(partial(r, zz, 1 - x))
            send(xss.at[r, i], xrs.at[r, i], beside, recv_index(("xs", r, i)))
            send(xs.at[r, i], xr.at[r, i], beside, recv_index(("x", r, i)))

    def project_own(r):
        for i, zz in enumerate(targets):
            own[r, i] = partial(r, zz, x)

    def x_sum(r, i):
        wait(xrs.at[r, i], recv_index(("xs", r, i)))
        wait(xr.at[r, i], recv_index(("x", r, i)))
        own[r, i] = own[r, i] + unpack(xr[r, i], xrs[r, i])

    def send_final(r, i, value, zz, kind):
        code, factor = pack(value)
        for core in range(2):
            fin[r, i, core] = code[:, core * chunk : (core + 1) * chunk]
            fins[r, i, core] = factor[:, core * chunk : (core + 1) * chunk]

    def start_final(r, i, zz, kind):
        for core in range(2):
            where = on_core(zz, core)
            send(fins.at[r, i, core], finrs.at[r, i], where, recv_index(("fs", r, i)), is_f)
            send(fin.at[r, i, core], finr.at[r, i], where, recv_index(("f", r, i)), is_f)

    def cross_first(r):
        x_sum(r, 0)

        def go():
            zls[r], zlss[r] = pack(own[r, 0])

        pl.when(is_o)(go)
        where = {"ctx": at(z_near, x)}
        send(zlss.at[r], zlrs.at[r], where, recv_index(("zls", r)), is_o)
        send(zls.at[r], zlr.at[r], where, recv_index(("zl", r)), is_o)

    def cross_second(r):
        wait(zlrs.at[r], recv_index(("zls", r)), is_f)
        wait(zlr.at[r], recv_index(("zl", r)), is_f)

        def go():
            send_final(r, 0, own[r, 0] + unpack(zlr[r], zlrs[r]), z_far, "cross")

        pl.when(is_f)(go)
        start_final(r, 0, z_far, "cross")

    def near_step(r):
        x_sum(r, 1)

        def keep():
            for core in range(2):

                def half():
                    mine[r] = own[r, 1, :, core * chunk : (core + 1) * chunk]
                    locs[r] = own[r, 1, :, (1 - core) * chunk : (2 - core) * chunk]

                pl.when(b == core)(half)

        pl.when(is_o)(keep)
        send(locs.at[r], locr.at[r], twin, recv_index(("loc", r)), is_o)
        pl.when(is_f)(lambda: send_final(r, 1, own[r, 1], z_near, "near"))
        start_final(r, 1, z_near, "near")

    def query(r):
        wait(locr.at[r], recv_index(("loc", r)), is_f)

        def take():
            mine[r] = locr[r]

        pl.when(is_f)(take)
        total = mine[r]
        for i in (1, 0):
            wait(finrs.at[r, i], recv_index(("fs", r, i)))
            wait(finr.at[r, i], recv_index(("f", r, i)))
            total = total + unpack(finr[r, i], finrs[r, i])
        q = total.astype(bf16)
        for j in range(2):
            qb[0, r, j * rp : (j + 1) * rp, :] = q[:, j * HD : (j + 1) * HD]
        send(qb.at[0, r], qb.at[1, r], beside, recv_index(("q", r)))

    place = lax.broadcasted_iota(i32, (span, 2 * rp), 0)

    def attend(i, r):
        part = slice(r * rp, (r + 1) * rp)
        if i == 1:
            wait(qb.at[1, r], recv_index(("q", r)))
        home_r = jnp.concatenate([home[:, part]] * 2, axis=1)
        lens_r = jnp.concatenate([lens[:, part]] * 2, axis=1)
        top = jnp.full((1, 2 * rp), -1e30, f32)
        for s in range(Z):
            block = at(s, x)
            limit = jnp.where(home_r == block, span, lens_r - block * span)
            raw = lax.dot_general(kv[0, s], qb[i, r], (((1,), (1,)), ((), ())), preferred_element_type=f32)
            raw = jnp.where(place < limit, raw, -1e30)
            sc[s] = raw
            top = jnp.maximum(top, jnp.max(raw, axis=0, keepdims=True))
        tot = jnp.zeros((1, 2 * rp), f32)
        acc_o = jnp.zeros((HD, 2 * rp), f32)
        for s in range(Z):
            e = jnp.exp((sc[s] - top) * scale)
            tot = tot + jnp.sum(e, axis=0, keepdims=True)
            acc_o = acc_o + jnp.dot(vt[s], e.astype(bf16), preferred_element_type=f32)
        if i == 0:
            os_[r] = acc_o
            st[r, 0:1, :] = top
            st[r, 1:2, :] = tot
        else:
            code, factor = pack(acc_o)
            oqs[r] = code
            oss[r, 0:1, :] = top
            oss[r, 1:2, :] = tot
            oss[r, 2:3, :] = factor
            oss[r, 3:4, :] = factor
            send(oss.at[r], osr.at[r], beside, recv_index(("os", r)))
            send(oqs.at[r], oqr.at[r], beside, recv_index(("o", r)))

    ag_sem = [recv_index(("ag", r), 8) for r in range(PARTS)]

    def slot(zz, xx, core):
        return zz * 4 + xx * 2 + core

    def merge(r):
        wait(osr.at[r], recv_index(("os", r)))
        wait(oqr.at[r], recv_index(("o", r)))
        m0, m1 = st[r, 0:1, :], osr[r, 0:1, :]
        l0, l1 = st[r, 1:2, :], osr[r, 1:2, :]
        m = jnp.maximum(m0, m1)
        a0, a1 = jnp.exp((m0 - m) * scale), jnp.exp((m1 - m) * scale)
        res = (a0 * os_[r] + unpack(oqr[r], a1 * osr[r, 2:3, :])) / (a0 * l0 + a1 * l1)
        turned = res.T.astype(bf16)
        for j in range(2):
            az[r, :, j * HD : (j + 1) * HD] = turned[j * rp : (j + 1) * rp, :]
        mine_slot = slot(zh, x, b)

        def keep():
            ag[r, mine_slot] = az[r]

        pl.when(is_o)(keep)
        send(az.at[r], ag.at[r, mine_slot], twin, ag_sem[r] + mine_slot, is_f)
        for zz in (z_far, z_two, z_near):
            send(az.at[r], ag.at[r, mine_slot], on_core(zz, zb), ag_sem[r] + mine_slot)

    def product(r, s):
        first = pl.multiple_of(s * chunk, chunk)
        return jnp.dot(ag[r, s], wo[pl.ds(first, chunk), :], preferred_element_type=f32)

    def relay(r, zz, first=False):
        part = slice(r * rp, (r + 1) * rp)
        for core in range(2):
            s = slot(zz, x, core)
            if zz is near:
                wait(ag.at[r, s], ag_sem[r] + s, jnp.logical_not(jnp.logical_and(is_o, b == core)))
            else:
                wait(ag.at[r, s], ag_sem[r] + s)
            send(ag.at[r, s], ag.at[r, s], beside, ag_sem[r] + s)
        value = product(r, slot(zz, x, 0)) + product(r, slot(zz, x, 1))
        if first:
            acc[part, :] = value
        else:
            acc[part, :] += value

    def collect(r, zz):
        part = slice(r * rp, (r + 1) * rp)
        for core in range(2):
            s = slot(zz, 1 - x, core)
            wait(ag.at[r, s], ag_sem[r] + s)
        acc[part, :] += product(r, slot(zz, 1 - x, 0)) + product(r, slot(zz, 1 - x, 1))

    quarter = out.shape[0]

    def rows_of(t, core):
        return pl.ds(pl.multiple_of(t * 2 * quarter + core * quarter, quarter), quarter)

    def reduce_cores(t):
        send(acc.at[rows_of(t, 1 - b), :], cr.at[t], twin, recv_index(("c", t)))

    def reduce_chips(t):
        wait(cr.at[t], recv_index(("c", t)))

        def away():
            ys[...] = (acc[rows_of(t, b), :] + cr[t]).astype(bf16)

        pl.when(y != t)(away)
        send(ys, yr, over, recv_index("y"), y != t)

    def finish(t):
        def here():
            out[...] = acc[rows_of(t, b), :] + cr[t] + yr[...].astype(f32)

        wait(yr, recv_index("y"), y == t)
        pl.when(y == t)(here)

    normalise(0)
    loads[2].wait()
    project_out(0)
    give(z_far)
    give(z_two)
    normalise(1)
    project_out(1)
    give(z_near)
    project_own(0)
    project_own(1)
    cross_first(0)
    cross_second(0)
    near_step(0)
    share(z_near)
    cross_first(1)
    share(z_two)
    share(z_far)
    query(0)
    for cp in loads[3:]:
        cp.wait()
    for zz in (z_near, z_two, z_far):
        wait(kv.at[1 - b, zz], kvf_sem + zz)
    for s in range(Z):
        vt[s] = kv[1, s].astype(f32).T.astype(bf16)
    attend(0, 0)
    near_step(1)
    cross_second(1)
    attend(1, 0)
    query(1)
    attend(0, 1)
    merge(0)
    attend(1, 1)
    relay(0, near, True)
    relay(0, cross)
    merge(1)
    relay(1, near, True)
    collect(0, near)
    collect(0, cross)
    reduce_cores(0)
    relay(1, cross)
    reduce_chips(0)
    collect(1, near)
    collect(1, cross)
    reduce_cores(1)
    finish(0)
    reduce_chips(1)
    finish(1)
    for cond, cp in pending:
        run(cond, cp.wait_send)


def fused(hidden, norm_gain, w_query, keys, values, w_output, valid_len, home_block):
    rows, feat = hidden.shape
    cols = w_output.shape[1]
    nz, nh = lax.axis_size("ctx"), lax.axis_size("head")
    span = keys.shape[1]
    chunk = w_query.shape[1] // nz
    rp = rows // PARTS
    quarter = rows // nh
    hbm = pl.BlockSpec(memory_space=pltpu.HBM)
    return pl.pallas_call(
        fused_kernel,
        out_shape=jax.ShapeDtypeStruct((quarter, cols), f32),
        in_specs=[hbm] * 8,
        out_specs=pl.BlockSpec(memory_space=pltpu.VMEM),
        scratch_shapes=[
            pltpu.VMEM((rows, feat), bf16),
            pltpu.VMEM((1, feat), f32),
            pltpu.VMEM(w_query.shape, bf16),
            pltpu.VMEM(w_output.shape, bf16),
            pltpu.VMEM((1, rows), i32),
            pltpu.VMEM((1, rows), i32),
            pltpu.VMEM((2, Z, span, HD), bf16),
            pltpu.VMEM((Z, HD, span), bf16),
            pltpu.VMEM((rows, feat), bf16),
            pltpu.VMEM((nz, 8, 128), f32),
            pltpu.VMEM((PARTS, 2, rp, 2 * chunk), i16),
            pltpu.VMEM((PARTS, 2, 1, 2 * chunk), f32),
            pltpu.VMEM((PARTS, 2, rp, 2 * chunk), i16),
            pltpu.VMEM((PARTS, 2, 1, 2 * chunk), f32),
            pltpu.VMEM((PARTS, 2, rp, 2 * chunk), f32),
            pltpu.VMEM((PARTS, rp, 2 * chunk), i16),
            pltpu.VMEM((PARTS, 1, 2 * chunk), f32),
            pltpu.VMEM((PARTS, rp, 2 * chunk), i16),
            pltpu.VMEM((PARTS, 1, 2 * chunk), f32),
            pltpu.VMEM((PARTS, rp, chunk), f32),
            pltpu.VMEM((PARTS, rp, chunk), f32),
            pltpu.VMEM((PARTS, 2, 2, rp, chunk), i16),
            pltpu.VMEM((PARTS, 2, 2, 1, chunk), f32),
            pltpu.VMEM((PARTS, 2, rp, chunk), i16),
            pltpu.VMEM((PARTS, 2, 1, chunk), f32),
            pltpu.VMEM((PARTS, rp, chunk), f32),
            pltpu.VMEM((2, PARTS, 2 * rp, HD), bf16),
            pltpu.VMEM((Z, span, 2 * rp), f32),
            pltpu.VMEM((PARTS, HD, 2 * rp), f32),
            pltpu.VMEM((PARTS, 8, 2 * rp), f32),
            pltpu.VMEM((PARTS, HD, 2 * rp), i16),
            pltpu.VMEM((PARTS, 4, 2 * rp), f32),
            pltpu.VMEM((PARTS, HD, 2 * rp), i16),
            pltpu.VMEM((PARTS, 4, 2 * rp), f32),
            pltpu.VMEM((PARTS, rp, chunk), bf16),
            pltpu.VMEM((PARTS, nz, rp, chunk), bf16),
            pltpu.VMEM((rows, cols), f32),
            pltpu.VMEM((2, quarter, cols), f32),
            pltpu.VMEM((quarter, cols), bf16),
            pltpu.VMEM((quarter, cols), bf16),
            pltpu.SemaphoreType.DMA((8,)),
            pltpu.SemaphoreType.DMA((NSEM,)),
            pltpu.SemaphoreType.DMA((NSEM,)),
        ],
        compiler_params=pltpu.CompilerParams(
            collective_id=0, has_side_effects=True, vmem_limit_bytes=60 * 1024 * 1024
        ),
    )(
        hidden, norm_gain.reshape(1, -1), w_query, keys, values, w_output,
        valid_len.reshape(1, -1), home_block.reshape(1, -1),
    )


def shards(
    hidden, norm_gain, w_query, manifest_keys, manifest_values, w_output, valid_len, home_block
):
    ctx_count = lax.axis_size("ctx")
    ctx_index = lax.axis_index("ctx")
    head_index = lax.axis_index("head")
    rows, feat = hidden.shape
    d_model = feat * ctx_count
    width = w_query.shape[1]
    heads_here = width // HD
    group = H // KVH
    span = manifest_keys.shape[1]
    hsplit = min(ctx_count, heads_here)
    rsplit = ctx_count // hsplit
    rows_dev = rows // rsplit
    heads_dev = heads_here // hsplit

    widened = hidden.astype(jnp.float32)
    total_sq = lax.psum(jnp.sum(widened * widened, axis=1, keepdims=True), "ctx")
    inv_rms = lax.rsqrt(total_sq / d_model + 1e-05)
    gain = lax.dynamic_slice_in_dim(norm_gain, ctx_index * feat, feat, 0)
    normed = (widened * inv_rms * gain[None, :]).astype(jnp.bfloat16)
    partial = jnp.dot(normed, w_query, preferred_element_type=jnp.float32)
    partial = partial.reshape(rsplit, rows_dev, hsplit, heads_dev * HD).transpose(2, 0, 1, 3)
    partial = partial.reshape(ctx_count, rows_dev, heads_dev * HD)
    query = lax.psum_scatter(partial, "ctx", scatter_dimension=0, tiled=False).astype(jnp.bfloat16)

    dest_heads = head_index * heads_here + (jnp.arange(ctx_count) // rsplit) * heads_dev
    dest_kv = dest_heads // group
    kv = jnp.stack(
        [
            jnp.stack([lax.dynamic_index_in_dim(a, dest_kv[i], 0, keepdims=False) for a in (manifest_keys, manifest_values)])
            for i in range(ctx_count)
        ]
    )
    kv = lax.all_to_all(kv, "ctx", split_axis=0, concat_axis=0, tiled=True)
    kv = kv.transpose(1, 0, 2, 3).reshape(2, ctx_count * span, HD)
    keys, values = kv[0], kv[1]

    first_row = (ctx_index % rsplit) * rows_dev
    lens = lax.dynamic_slice_in_dim(valid_len, first_row, rows_dev, 0)
    blocks = lax.dynamic_slice_in_dim(home_block, first_row, rows_dev, 0)
    places = jnp.arange(ctx_count * span, dtype=jnp.int32)
    usable = (places[None, :] < lens[:, None]) | ((places // span)[None, :] == blocks[:, None])
    usable = usable[:, None, :]
    q3 = query.reshape(rows_dev, heads_dev, HD)
    scores = jnp.einsum("nhd,jd->nhj", q3, keys, preferred_element_type=jnp.float32) * (
        1.0 / math.sqrt(HD)
    )
    scores = jnp.where(usable, scores, -1e30)
    row_max = jnp.max(scores, axis=2, keepdims=True)
    expo = jnp.where(usable, jnp.exp(scores - row_max), 0.0)
    row_sum = jnp.sum(expo, axis=2, keepdims=True)
    weighted = jnp.einsum(
        "nhj,jd->nhd", expo.astype(jnp.bfloat16), values, preferred_element_type=jnp.float32
    )
    attn = (weighted / row_sum).astype(jnp.bfloat16).reshape(rows_dev, heads_dev * HD)
    attn = lax.all_gather(attn, "ctx", axis=0, tiled=False)
    attn = attn.reshape(hsplit, rsplit, rows_dev, heads_dev * HD).transpose(1, 2, 0, 3)
    attn = attn.reshape(rows, width)
    return lax.psum_scatter(
        jnp.dot(attn, w_output, preferred_element_type=jnp.float32),
        "head",
        scatter_dimension=0,
        tiled=True,
    )


def solution(mesh):
    in_specs = (
        P(None, "ctx"),
        P(),
        P("ctx", "head"),
        P(None, "ctx", None),
        P(None, "ctx", None),
        P("head", "ctx"),
        P(),
        P(),
    )
    out_specs = P("head", "ctx")
    small = mesh.shape["ctx"] == Z * X and mesh.shape["head"] * X == KVH
    return jax.shard_map(fused if small else shards, mesh=mesh, in_specs=in_specs, out_specs=out_specs, check_vma=False)
```

```python
import math

import jax
import jax.numpy as jnp
from jax import lax
from jax.experimental import pallas as pl
from jax.experimental.pallas import tpu as pltpu
from jax.sharding import PartitionSpec as P

H = 64
KVH = 8
HD = 128

Z = 4
X = 2
PARTS = 2
NSEM = 128

MESH = pl.DeviceIdType.MESH
f32, bf16, i16, i32 = jnp.float32, jnp.bfloat16, jnp.int16, jnp.int32


def fused_kernel(
    hidden_hbm, gain_hbm, wq_hbm, k_hbm, v_hbm, wo_hbm, lens_hbm, home_hbm, out,
    hid, gain, wq, wo, lens, home, kv, vt, nrm, sq,
    xs, xss, xr, xrs, own, zls, zlss, zlr, zlrs, locs, locr, fin, fins, finr, finrs, mine,
    qb, sc, os_, st, oqs, oss, oqr, osr, az, ag, acc, cr, ys, yr,
    local_sem, send_sem, recv_sem,
):
    c = lax.axis_index("ctx")
    h = lax.axis_index("head")
    z, x = lax.div(c, X), lax.rem(c, X)
    y, b = lax.div(h, 2), lax.rem(h, 2)
    zb, zh = lax.rem(z, 2), lax.div(z, 2)
    nz = lax.axis_size("ctx")
    rows, feat = hid.shape
    rp = rows // PARTS
    span = kv.shape[2]
    chunk = wq.shape[1] // nz
    scale = 1.0 / math.sqrt(HD)
    is_o = b == zb
    is_f = b != zb
    pending = []
    sems = {"send": 0, "recv": 0}
    names = {}

    def at(zz, xx):
        return zz * X + xx

    def recv_index(name, count=1):
        if name not in names:
            names[name] = sems["recv"]
            sems["recv"] += count
        return names[name]

    def run(cond, fn):
        if cond is None:
            fn()
        else:
            pl.when(cond)(fn)

    def send(src, dst, where, recv, cond=None):
        i = sems["send"]
        sems["send"] += 1
        copy = pltpu.make_async_remote_copy(
            src_ref=src, dst_ref=dst, send_sem=send_sem.at[i], recv_sem=recv_sem.at[recv],
            device_id=where, device_id_type=MESH,
        )
        run(cond, copy.start)
        pending.append((cond, copy))

    def wait(dst, recv, cond=None):
        copy = pltpu.make_async_remote_copy(
            src_ref=dst, dst_ref=dst, send_sem=send_sem.at[0], recv_sem=recv_sem.at[recv],
            device_id={"ctx": at(z, 1 - x)}, device_id_type=MESH,
        )
        run(cond, copy.wait_recv)

    beside = {"ctx": at(z, 1 - x)}
    twin = {"head": y * 2 + 1 - b}
    over = {"head": (1 - y) * 2 + b}

    def key_head(zz):
        return 4 * y + 2 * lax.rem(zz, 2) + lax.div(zz, 2)

    z_near = z + 1 - 2 * zb
    z_far = 3 - z
    z_two = lax.rem(z + 2, Z)

    def on_core(zz, core):
        return {"ctx": at(zz, x), "head": y * 2 + core}

    loads = [
        pltpu.make_async_copy(hidden_hbm, hid, local_sem.at[0]),
        pltpu.make_async_copy(gain_hbm.at[:, pl.ds(pl.multiple_of(c * feat, feat), feat)], gain, local_sem.at[1]),
        pltpu.make_async_copy(wq_hbm, wq, local_sem.at[2]),
        pltpu.make_async_copy(k_hbm.at[key_head(z)], kv.at[0, z], local_sem.at[3]),
        pltpu.make_async_copy(v_hbm.at[key_head(z)], kv.at[1, z], local_sem.at[4]),
        pltpu.make_async_copy(lens_hbm, lens, local_sem.at[5]),
        pltpu.make_async_copy(home_hbm, home, local_sem.at[6]),
        pltpu.make_async_copy(wo_hbm, wo, local_sem.at[7]),
    ]
    for cp in loads:
        cp.start()

    barrier = pltpu.get_barrier_semaphore()
    peers = [{"ctx": lax.rem(c + k, nz)} for k in range(1, nz)]
    peers += [on_core(zz, 1 - b) for zz in (z_near, z_far, z_two)]
    peers += [twin, over]
    for peer in peers:
        pl.semaphore_signal(barrier, inc=1, device_id=peer, device_id_type=MESH)

    loads[0].wait()
    eye = lax.broadcasted_iota(i32, (128, 128), 0) == lax.broadcasted_iota(i32, (128, 128), 1)
    wide = hid[...].astype(f32)
    col = jnp.sum(wide * wide, axis=1, keepdims=True)
    pieces = [
        jnp.sum(jnp.where(eye, col[i * 128 : (i + 1) * 128], 0.0), axis=0, keepdims=True)
        for i in range(rows // 128)
    ]
    pieces.append(jnp.zeros((8 - rows // 128, 128), f32))
    sq[0] = jnp.concatenate(pieces, axis=0)
    pl.semaphore_wait(barrier, len(peers))
    sq_sem = recv_index("sq", nz)
    for k in range(1, nz):
        send(sq.at[0], sq.at[k], {"ctx": lax.rem(c + k, nz)}, sq_sem + k)

    kv_sem = recv_index("kv", Z)
    kvf_sem = recv_index("kvf", Z)
    def give(zz):
        for core, hbm in ((0, k_hbm), (1, v_hbm)):
            send(hbm.at[key_head(zz)], kv.at[core, z], {"ctx": at(zz, x)}, kv_sem + z, b == core)

    def share(zz):
        wait(kv.at[b, zz], kv_sem + zz)
        send(kv.at[b, zz], kv.at[b, zz], twin, kvf_sem + zz)

    loads[1].wait()
    for k in range(1, nz):
        wait(sq.at[k], sq_sem + k)
    total = sq[0]
    for k in range(1, nz):
        total = total + sq[k]
    inv = lax.rsqrt(total / (feat * nz) + 1e-05)

    def normalise(i):
        part = slice(i * 128, (i + 1) * 128)
        inv_col = jnp.sum(jnp.where(eye, inv[i : i + 1, :], 0.0), axis=1, keepdims=True)
        nrm[part, :] = (hid[part, :].astype(f32) * inv_col * gain[...]).astype(bf16)

    def pack(value):
        top = jnp.maximum(jnp.max(jnp.abs(value), axis=0, keepdims=True), 1e-30)
        code = jnp.round(value * (32766.0 / top)).astype(i32).astype(i16)
        return code, top * (1.0 / 32766.0)

    def unpack(code, factor):
        return code.astype(i32).astype(f32) * factor

    cross, near = 1 - zh, zh
    targets = (cross, near)

    def partial(r, zz, xx):
        first = pl.multiple_of(zz * 4 * chunk + xx * 2 * chunk, 2 * chunk)
        return jnp.dot(nrm[r * rp : (r + 1) * rp, :], wq[:, pl.ds(first, 2 * chunk)], preferred_element_type=f32)

    def project_out(r):
        for i, zz in enumerate(targets):
            xs[r, i], xss[r, i] = pack(partial(r, zz, 1 - x))
            send(xss.at[r, i], xrs.at[r, i], beside, recv_index(("xs", r, i)))
            send(xs.at[r, i], xr.at[r, i], beside, recv_index(("x", r, i)))

    def project_own(r):
        for i, zz in enumerate(targets):
            own[r, i] = partial(r, zz, x)

    def x_sum(r, i):
        wait(xrs.at[r, i], recv_index(("xs", r, i)))
        wait(xr.at[r, i], recv_index(("x", r, i)))
        own[r, i] = own[r, i] + unpack(xr[r, i], xrs[r, i])

    def send_final(r, i, value, zz, kind):
        code, factor = pack(value)
        for core in range(2):
            fin[r, i, core] = code[:, core * chunk : (core + 1) * chunk]
            fins[r, i, core] = factor[:, core * chunk : (core + 1) * chunk]

    def start_final(r, i, zz, kind):
        for core in range(2):
            where = on_core(zz, core)
            send(fins.at[r, i, core], finrs.at[r, i], where, recv_index(("fs", r, i)), is_f)
            send(fin.at[r, i, core], finr.at[r, i], where, recv_index(("f", r, i)), is_f)

    def cross_first(r):
        x_sum(r, 0)

        def go():
            zls[r], zlss[r] = pack(own[r, 0])

        pl.when(is_o)(go)
        where = {"ctx": at(z_near, x)}
        send(zlss.at[r], zlrs.at[r], where, recv_index(("zls", r)), is_o)
        send(zls.at[r], zlr.at[r], where, recv_index(("zl", r)), is_o)

    def cross_second(r):
        wait(zlrs.at[r], recv_index(("zls", r)), is_f)
        wait(zlr.at[r], recv_index(("zl", r)), is_f)

        def go():
            send_final(r, 0, own[r, 0] + unpack(zlr[r], zlrs[r]), z_far, "cross")

        pl.when(is_f)(go)
        start_final(r, 0, z_far, "cross")

    def near_step(r):
        x_sum(r, 1)

        def keep():
            for core in range(2):

                def half():
                    mine[r] = own[r, 1, :, core * chunk : (core + 1) * chunk]
                    locs[r] = own[r, 1, :, (1 - core) * chunk : (2 - core) * chunk]

                pl.when(b == core)(half)

        pl.when(is_o)(keep)
        send(locs.at[r], locr.at[r], twin, recv_index(("loc", r)), is_o)
        pl.when(is_f)(lambda: send_final(r, 1, own[r, 1], z_near, "near"))
        start_final(r, 1, z_near, "near")

    def query(r):
        wait(locr.at[r], recv_index(("loc", r)), is_f)

        def take():
            mine[r] = locr[r]

        pl.when(is_f)(take)
        total = mine[r]
        for i in (1, 0):
            wait(finrs.at[r, i], recv_index(("fs", r, i)))
            wait(finr.at[r, i], recv_index(("f", r, i)))
            total = total + unpack(finr[r, i], finrs[r, i])
        q = total.astype(bf16)
        for j in range(2):
            qb[0, r, j * rp : (j + 1) * rp, :] = q[:, j * HD : (j + 1) * HD]
        send(qb.at[0, r], qb.at[1, r], beside, recv_index(("q", r)))

    place = lax.broadcasted_iota(i32, (span, 2 * rp), 0)

    def attend(i, r):
        part = slice(r * rp, (r + 1) * rp)
        if i == 1:
            wait(qb.at[1, r], recv_index(("q", r)))
        home_r = jnp.concatenate([home[:, part]] * 2, axis=1)
        lens_r = jnp.concatenate([lens[:, part]] * 2, axis=1)
        top = jnp.full((1, 2 * rp), -1e30, f32)
        for s in range(Z):
            block = at(s, x)
            limit = jnp.where(home_r == block, span, lens_r - block * span)
            raw = lax.dot_general(kv[0, s], qb[i, r], (((1,), (1,)), ((), ())), preferred_element_type=f32)
            raw = jnp.where(place < limit, raw, -1e30)
            sc[s] = raw
            top = jnp.maximum(top, jnp.max(raw, axis=0, keepdims=True))
        tot = jnp.zeros((1, 2 * rp), f32)
        acc_o = jnp.zeros((HD, 2 * rp), f32)
        for s in range(Z):
            e = jnp.exp((sc[s] - top) * scale)
            tot = tot + jnp.sum(e, axis=0, keepdims=True)
            acc_o = acc_o + jnp.dot(vt[s], e.astype(bf16), preferred_element_type=f32)
        if i == 0:
            os_[r] = acc_o
            st[r, 0:1, :] = top
            st[r, 1:2, :] = tot
        else:
            code, factor = pack(acc_o)
            oqs[r] = code
            oss[r, 0:1, :] = top
            oss[r, 1:2, :] = tot
            oss[r, 2:3, :] = factor
            oss[r, 3:4, :] = factor
            send(oss.at[r], osr.at[r], beside, recv_index(("os", r)))
            send(oqs.at[r], oqr.at[r], beside, recv_index(("o", r)))

    ag_sem = [recv_index(("ag", r), 8) for r in range(PARTS)]

    def slot(zz, xx, core):
        return zz * 4 + xx * 2 + core

    def merge(r):
        wait(osr.at[r], recv_index(("os", r)))
        wait(oqr.at[r], recv_index(("o", r)))
        m0, m1 = st[r, 0:1, :], osr[r, 0:1, :]
        l0, l1 = st[r, 1:2, :], osr[r, 1:2, :]
        m = jnp.maximum(m0, m1)
        a0, a1 = jnp.exp((m0 - m) * scale), jnp.exp((m1 - m) * scale)
        res = (a0 * os_[r] + unpack(oqr[r], a1 * osr[r, 2:3, :])) / (a0 * l0 + a1 * l1)
        turned = res.T.astype(bf16)
        for j in range(2):
            az[r, :, j * HD : (j + 1) * HD] = turned[j * rp : (j + 1) * rp, :]
        mine_slot = slot(zh, x, b)

        def keep():
            ag[r, mine_slot] = az[r]

        pl.when(is_o)(keep)
        send(az.at[r], ag.at[r, mine_slot], twin, ag_sem[r] + mine_slot, is_f)
        for zz in (z_far, z_two, z_near):
            send(az.at[r], ag.at[r, mine_slot], on_core(zz, zb), ag_sem[r] + mine_slot)

    def product(r, s):
        first = pl.multiple_of(s * chunk, chunk)
        return jnp.dot(ag[r, s], wo[pl.ds(first, chunk), :], preferred_element_type=f32)

    def relay(r, zz):
        for core in range(2):
            s = slot(zz, x, core)
            if zz is near:
                wait(ag.at[r, s], ag_sem[r] + s, jnp.logical_not(jnp.logical_and(is_o, b == core)))
            else:
                wait(ag.at[r, s], ag_sem[r] + s)
            send(ag.at[r, s], ag.at[r, s], beside, ag_sem[r] + s)

    def multiply(r, zz, first=False):
        part = slice(r * rp, (r + 1) * rp)
        value = product(r, slot(zz, x, 0)) + product(r, slot(zz, x, 1))
        if first:
            acc[part, :] = value
        else:
            acc[part, :] += value

    def collect(r, zz):
        part = slice(r * rp, (r + 1) * rp)
        for core in range(2):
            s = slot(zz, 1 - x, core)
            wait(ag.at[r, s], ag_sem[r] + s)
        acc[part, :] += product(r, slot(zz, 1 - x, 0)) + product(r, slot(zz, 1 - x, 1))

    quarter = out.shape[0]

    def rows_of(t, core):
        return pl.ds(pl.multiple_of(t * 2 * quarter + core * quarter, quarter), quarter)

    def columns(k):
        return slice(k * out.shape[1] // 2, (k + 1) * out.shape[1] // 2)

    def reduce_cores(t):
        for k in range(2):
            send(acc.at[rows_of(t, 1 - b), columns(k)], cr.at[t, :, columns(k)], twin, recv_index(("c", t, k)))

    def reduce_chips(t):
        for k in range(2):
            part = columns(k)
            wait(cr.at[t, :, part], recv_index(("c", t, k)))

            def away():
                ys[:, part] = (acc[rows_of(t, b), part] + cr[t, :, part]).astype(bf16)

            pl.when(y != t)(away)
            send(ys.at[:, part], yr.at[:, part], over, recv_index(("y", k)), y != t)

    def finish(t):
        for k in range(2):
            part = columns(k)

            def here():
                out[:, part] = acc[rows_of(t, b), part] + cr[t, :, part] + yr[:, part].astype(f32)

            wait(yr.at[:, part], recv_index(("y", k)), y == t)
            pl.when(y == t)(here)

    normalise(0)
    loads[2].wait()
    project_out(0)
    give(z_far)
    give(z_two)
    normalise(1)
    project_out(1)
    give(z_near)
    project_own(0)
    project_own(1)
    cross_first(0)
    cross_second(0)
    near_step(0)
    share(z_near)
    cross_first(1)
    share(z_two)
    share(z_far)
    query(0)
    near_step(1)
    cross_second(1)
    for cp in loads[3:]:
        cp.wait()
    for zz in (z_near, z_two, z_far):
        wait(kv.at[1 - b, zz], kvf_sem + zz)
    for s in range(Z):
        vt[s] = kv[1, s].astype(f32).T.astype(bf16)
    attend(0, 0)
    attend(1, 0)
    query(1)
    attend(0, 1)
    merge(0)
    attend(1, 1)
    relay(0, near)
    merge(1)
    relay(0, cross)
    relay(1, near)
    multiply(0, near, True)
    multiply(0, cross)
    multiply(1, near, True)
    collect(0, near)
    collect(0, cross)
    reduce_cores(0)
    relay(1, cross)
    multiply(1, cross)
    reduce_chips(0)
    collect(1, near)
    collect(1, cross)
    reduce_cores(1)
    finish(0)
    reduce_chips(1)
    finish(1)
    for cond, cp in pending:
        run(cond, cp.wait_send)


def fused(hidden, norm_gain, w_query, keys, values, w_output, valid_len, home_block):
    rows, feat = hidden.shape
    cols = w_output.shape[1]
    nz, nh = lax.axis_size("ctx"), lax.axis_size("head")
    span = keys.shape[1]
    chunk = w_query.shape[1] // nz
    rp = rows // PARTS
    quarter = rows // nh
    hbm = pl.BlockSpec(memory_space=pltpu.HBM)
    return pl.pallas_call(
        fused_kernel,
        out_shape=jax.ShapeDtypeStruct((quarter, cols), f32),
        in_specs=[hbm] * 8,
        out_specs=pl.BlockSpec(memory_space=pltpu.VMEM),
        scratch_shapes=[
            pltpu.VMEM((rows, feat), bf16),
            pltpu.VMEM((1, feat), f32),
            pltpu.VMEM(w_query.shape, bf16),
            pltpu.VMEM(w_output.shape, bf16),
            pltpu.VMEM((1, rows), i32),
            pltpu.VMEM((1, rows), i32),
            pltpu.VMEM((2, Z, span, HD), bf16),
            pltpu.VMEM((Z, HD, span), bf16),
            pltpu.VMEM((rows, feat), bf16),
            pltpu.VMEM((nz, 8, 128), f32),
            pltpu.VMEM((PARTS, 2, rp, 2 * chunk), i16),
            pltpu.VMEM((PARTS, 2, 1, 2 * chunk), f32),
            pltpu.VMEM((PARTS, 2, rp, 2 * chunk), i16),
            pltpu.VMEM((PARTS, 2, 1, 2 * chunk), f32),
            pltpu.VMEM((PARTS, 2, rp, 2 * chunk), f32),
            pltpu.VMEM((PARTS, rp, 2 * chunk), i16),
            pltpu.VMEM((PARTS, 1, 2 * chunk), f32),
            pltpu.VMEM((PARTS, rp, 2 * chunk), i16),
            pltpu.VMEM((PARTS, 1, 2 * chunk), f32),
            pltpu.VMEM((PARTS, rp, chunk), f32),
            pltpu.VMEM((PARTS, rp, chunk), f32),
            pltpu.VMEM((PARTS, 2, 2, rp, chunk), i16),
            pltpu.VMEM((PARTS, 2, 2, 1, chunk), f32),
            pltpu.VMEM((PARTS, 2, rp, chunk), i16),
            pltpu.VMEM((PARTS, 2, 1, chunk), f32),
            pltpu.VMEM((PARTS, rp, chunk), f32),
            pltpu.VMEM((2, PARTS, 2 * rp, HD), bf16),
            pltpu.VMEM((Z, span, 2 * rp), f32),
            pltpu.VMEM((PARTS, HD, 2 * rp), f32),
            pltpu.VMEM((PARTS, 8, 2 * rp), f32),
            pltpu.VMEM((PARTS, HD, 2 * rp), i16),
            pltpu.VMEM((PARTS, 4, 2 * rp), f32),
            pltpu.VMEM((PARTS, HD, 2 * rp), i16),
            pltpu.VMEM((PARTS, 4, 2 * rp), f32),
            pltpu.VMEM((PARTS, rp, chunk), bf16),
            pltpu.VMEM((PARTS, nz, rp, chunk), bf16),
            pltpu.VMEM((rows, cols), f32),
            pltpu.VMEM((2, quarter, cols), f32),
            pltpu.VMEM((quarter, cols), bf16),
            pltpu.VMEM((quarter, cols), bf16),
            pltpu.SemaphoreType.DMA((8,)),
            pltpu.SemaphoreType.DMA((NSEM,)),
            pltpu.SemaphoreType.DMA((NSEM,)),
        ],
        compiler_params=pltpu.CompilerParams(
            collective_id=0, has_side_effects=True, vmem_limit_bytes=60 * 1024 * 1024
        ),
    )(
        hidden, norm_gain.reshape(1, -1), w_query, keys, values, w_output,
        valid_len.reshape(1, -1), home_block.reshape(1, -1),
    )


def shards(
    hidden, norm_gain, w_query, manifest_keys, manifest_values, w_output, valid_len, home_block
):
    ctx_count = lax.axis_size("ctx")
    ctx_index = lax.axis_index("ctx")
    head_index = lax.axis_index("head")
    rows, feat = hidden.shape
    d_model = feat * ctx_count
    width = w_query.shape[1]
    heads_here = width // HD
    group = H // KVH
    span = manifest_keys.shape[1]
    hsplit = min(ctx_count, heads_here)
    rsplit = ctx_count // hsplit
    rows_dev = rows // rsplit
    heads_dev = heads_here // hsplit

    widened = hidden.astype(jnp.float32)
    total_sq = lax.psum(jnp.sum(widened * widened, axis=1, keepdims=True), "ctx")
    inv_rms = lax.rsqrt(total_sq / d_model + 1e-05)
    gain = lax.dynamic_slice_in_dim(norm_gain, ctx_index * feat, feat, 0)
    normed = (widened * inv_rms * gain[None, :]).astype(jnp.bfloat16)
    partial = jnp.dot(normed, w_query, preferred_element_type=jnp.float32)
    partial = partial.reshape(rsplit, rows_dev, hsplit, heads_dev * HD).transpose(2, 0, 1, 3)
    partial = partial.reshape(ctx_count, rows_dev, heads_dev * HD)
    query = lax.psum_scatter(partial, "ctx", scatter_dimension=0, tiled=False).astype(jnp.bfloat16)

    dest_heads = head_index * heads_here + (jnp.arange(ctx_count) // rsplit) * heads_dev
    dest_kv = dest_heads // group
    kv = jnp.stack(
        [
            jnp.stack([lax.dynamic_index_in_dim(a, dest_kv[i], 0, keepdims=False) for a in (manifest_keys, manifest_values)])
            for i in range(ctx_count)
        ]
    )
    kv = lax.all_to_all(kv, "ctx", split_axis=0, concat_axis=0, tiled=True)
    kv = kv.transpose(1, 0, 2, 3).reshape(2, ctx_count * span, HD)
    keys, values = kv[0], kv[1]

    first_row = (ctx_index % rsplit) * rows_dev
    lens = lax.dynamic_slice_in_dim(valid_len, first_row, rows_dev, 0)
    blocks = lax.dynamic_slice_in_dim(home_block, first_row, rows_dev, 0)
    places = jnp.arange(ctx_count * span, dtype=jnp.int32)
    usable = (places[None, :] < lens[:, None]) | ((places // span)[None, :] == blocks[:, None])
    usable = usable[:, None, :]
    q3 = query.reshape(rows_dev, heads_dev, HD)
    scores = jnp.einsum("nhd,jd->nhj", q3, keys, preferred_element_type=jnp.float32) * (
        1.0 / math.sqrt(HD)
    )
    scores = jnp.where(usable, scores, -1e30)
    row_max = jnp.max(scores, axis=2, keepdims=True)
    expo = jnp.where(usable, jnp.exp(scores - row_max), 0.0)
    row_sum = jnp.sum(expo, axis=2, keepdims=True)
    weighted = jnp.einsum(
        "nhj,jd->nhd", expo.astype(jnp.bfloat16), values, preferred_element_type=jnp.float32
    )
    attn = (weighted / row_sum).astype(jnp.bfloat16).reshape(rows_dev, heads_dev * HD)
    attn = lax.all_gather(attn, "ctx", axis=0, tiled=False)
    attn = attn.reshape(hsplit, rsplit, rows_dev, heads_dev * HD).transpose(1, 2, 0, 3)
    attn = attn.reshape(rows, width)
    return lax.psum_scatter(
        jnp.dot(attn, w_output, preferred_element_type=jnp.float32),
        "head",
        scatter_dimension=0,
        tiled=True,
    )


def solution(mesh):
    in_specs = (
        P(None, "ctx"),
        P(),
        P("ctx", "head"),
        P(None, "ctx", None),
        P(None, "ctx", None),
        P("head", "ctx"),
        P(),
        P(),
    )
    out_specs = P("head", "ctx")
    small = mesh.shape["ctx"] == Z * X and mesh.shape["head"] * X == KVH
    return jax.shard_map(fused if small else shards, mesh=mesh, in_specs=in_specs, out_specs=out_specs, check_vma=False)
```
